512 devices in a mesh: row: 16 (over y_lo, x, core), col: 32 (over z, y_hi).
Axes of the slice: x: 4, y: 8 (y_hi: 4, y_lo: 2; y = y_hi * 2 + y_lo), z: 8, core: 2. Of those that a mesh axis runs over, the one named last changes fastest.
Arguments:
- act_values: bfloat16 [2048, 16384], P('col', 'row'), may hold values from -6 to 6
- act_scales: float32 [2048, 128], P('col', 'row'), may hold values from 0.3 to 4
- grad_values: bfloat16 [2048, 28672], P('row', 'col'), may hold values from -6 to 6
- grad_scales: float32 [2048, 224], P('row', 'col'), may hold values from 0.3 to 4
- weight: bfloat16 [16384, 28672], P('row', 'col'), may hold values from -0.03125 to 0.03125
Outputs:
- input_grad: bfloat16 [2048, 16384], P('col', 'row')
- weight_grad: bfloat16 [16384, 28672], P('row', 'col')
The draws below stay inside these ranges and needn't reach their ends.
All inputs are finite; a program needn't handle non-finite values.
Results may differ from the reference program's by a relative error of at most 0.015.
Values may be sent and summed in bfloat16 or wider, within the bound.
No kernel may reach another device: no remote copies, remote signals or barrier semaphores. Data moves between devices by JAX's collectives and lax.ppermute only.
A program may use at most 64 MiB of HBM per device.

```python
import math
import jax
import jax.numpy as jnp
from jax import lax

D = 16384
FF = 28672
QB = 128
TOKENS = 2048
N_COL = 32


def with_spikes(drawn, rng, source, target, parts, factor):
    owner, partner = [(jnp.arange(drawn.shape[dim]) // (drawn.shape[dim] // parts)).reshape([-1 if axis == dim else 1 for axis in range(drawn.ndim)]) for dim in (source, target)]
    chosen = jax.random.permutation(rng, parts)[partner]
    strong = (owner == chosen) | (owner == (partner + parts // 2) % parts)
    return jnp.where(strong, factor * drawn, drawn)


def block_levels(rng, dims, shards, least, top_value):
    loudness = 1.0
    for position, parts in shards:
        heights = jax.random.uniform(jax.random.fold_in(jax.random.fold_in(rng, 6), position), (parts,), jnp.float32, least / len(shards), top_value / len(shards))
        loudness = loudness * jnp.repeat(jnp.exp(heights), dims[position] // parts).reshape((-1,) + (1,) * (len(dims) - 1 - position))
    return loudness


def scatter_about(key, dims, scale, reach, cuts=(), kind=jnp.bfloat16):
    array = jax.random.normal(key, dims, jnp.float32) * scale
    if len(cuts) > 0:
        array = block_levels(key, dims, cuts, -0.22, 0.18) * array
    return jnp.clip(array, min=-reach, max=reach).astype(kind)


def gaussian_with(own_key, extent, width, most, cuts, heavy, kind=jnp.bfloat16):
    values = width * jax.random.normal(own_key, extent, jnp.float32)
    if cuts:
        values = values * block_levels(own_key, extent, cuts, -0.22, 0.18)
    return jnp.clip(with_spikes(values, jax.random.fold_in(own_key, 3), *heavy), -most, most).astype(kind)


def setup_inputs(seed: int = 0) -> dict:
    keys = jax.random.split(jax.random.key(seed), 6)
    return {
        "act_values": scatter_about(keys[0], (TOKENS, D), 1.0, 6.0, ((0, 32), (1, 16))),
        "act_scales": jnp.clip(jnp.exp(math.log(4.0) - 2.5902671 * jax.random.uniform(keys[1], (TOKENS, D // QB), jnp.float32) ** block_levels(keys[1], (TOKENS, D // QB), ((0, 32), (1, 16)), -0.2, 0.2)), 0.3, 4.0),
        "grad_values": gaussian_with(keys[2], (TOKENS, FF), 1.0, 6.0, ((0, 16), (1, 32)), (1, 0, 32, 2.75)),
        "grad_scales": jnp.clip(jnp.exp(math.log(4.0) - 2.5902671 * jax.random.uniform(keys[3], (TOKENS, FF // QB), jnp.float32) ** block_levels(keys[3], (TOKENS, FF // QB), ((0, 16), (1, 32)), -0.2, 0.2)), 0.3, 4.0),
        "weight": scatter_about(keys[4], (D, FF), FF ** -0.5, 0.03125, ((0, 16), (1, 32))),
    }


def dequantize(values, scales):
    height, breadth = values.shape
    scaled = values.astype(jnp.float32).reshape(height, breadth // QB, QB) * scales[:, :, None]
    return scaled.reshape(height, breadth).astype(jnp.bfloat16)


def reference(act_values, act_scales, grad_values, grad_scales, weight):
    activations = dequantize(act_values, act_scales)
    gradients = dequantize(grad_values, grad_scales)
    weight_grad = lax.dot_general(activations, gradients, (((0,), (0,)), ((), ())), preferred_element_type=jnp.float32).astype(jnp.bfloat16)
    slab_width = FF // N_COL

    def accumulate(running, column):
        offset = column * slab_width
        grad_slab = lax.dynamic_slice_in_dim(gradients, offset, slab_width, 1)
        weight_slab = lax.dynamic_slice_in_dim(weight, offset, slab_width, 1)
        partial_block = lax.dot_general(grad_slab, weight_slab, (((1,), (1,)), ((), ())), preferred_element_type=jnp.float32).astype(jnp.bfloat16)
        partial_block = lax.optimization_barrier(partial_block)
        return running + partial_block.astype(jnp.float32), None

    summed, _ = lax.scan(accumulate, jnp.zeros((TOKENS, D), jnp.float32), jnp.arange(N_COL, dtype=jnp.int32))
    return summed.astype(jnp.bfloat16), weight_grad
```

```python
import jax
import jax.numpy as jnp
from jax import lax
from jax.experimental import pallas as pl
from jax.experimental.pallas import tpu as pltpu
from jax.sharding import Mesh, PartitionSpec as P


QB = 128
NY = 4
NZ = 8
ROW = ("ylo", "x", "core")
COL = ("z", "yhi")


def dequantize(values, scales):
    height, breadth = values.shape
    scaled = values.astype(jnp.float32).reshape(height, breadth // QB, QB) * scales[:, :, None]
    return scaled.reshape(height, breadth).astype(jnp.bfloat16)


def shift(array, axis, size, by):
    return lax.ppermute(array, axis, [(i, (i + by) % size) for i in range(size)])


def partial_kernel(grad_ref, weight_ref, out_ref):
    out_ref[...] = lax.dot_general(
        grad_ref[...], weight_ref[...], (((1,), (1,)), ((), ())), preferred_element_type=jnp.float32
    ).astype(out_ref.dtype)


def partial_product(gradients, weight, tile=256):
    tokens, hidden = gradients.shape
    width = weight.shape[0]
    return pl.pallas_call(
        partial_kernel,
        grid=(tokens // tile,),
        in_specs=[
            pl.BlockSpec((tile, hidden), lambda i: (i, 0)),
            pl.BlockSpec((width, hidden), lambda i: (0, 0)),
        ],
        out_specs=pl.BlockSpec((tile, width), lambda i: (i, 0)),
        out_shape=jax.ShapeDtypeStruct((tokens, width), jnp.bfloat16),
        cost_estimate=pl.CostEstimate(
            flops=2 * tokens * hidden * width,
            bytes_accessed=2 * (tokens * hidden + hidden * width + tokens * width),
            transcendentals=0,
        ),
        name="partial_product",
    )(gradients, weight)


def mark_kernel(*refs):
    refs[-1][...] = jnp.zeros_like(refs[-1])


def mark(*arrays):
    return pl.pallas_call(
        mark_kernel,
        in_specs=[pl.BlockSpec(memory_space=pl.ANY)] * len(arrays),
        out_shape=jax.ShapeDtypeStruct((8, 128), jnp.float32),
        cost_estimate=pl.CostEstimate(flops=0, bytes_accessed=4096, transcendentals=0),
        name="mark",
    )(*arrays)


def outer_kernel(places, z_ref, grad_ref, *refs):
    out_ref = refs[-1]
    z = z_ref[0]
    total = None
    for (hop, first, rows), act_ref in zip(places, refs[:-1]):
        start = ((z + hop) & (NZ - 1)) * (grad_ref.shape[0] // NZ) + first
        grads = grad_ref[pl.ds(pl.multiple_of(start, rows), rows), :]
        term = lax.dot_general(
            act_ref[...], grads, (((0,), (0,)), ((), ())), preferred_element_type=jnp.float32
        )
        total = term if total is None else total + term
    out_ref[...] = total.astype(out_ref.dtype)


def outer_product(held, gradients, z, marks, tile=256):
    tokens, hidden = gradients.shape
    width = held[0][1].shape[1]
    places = tuple(place for place, _ in held)
    arrays = [array for _, array in held]

    def kernel(*refs):
        outer_kernel(places, *refs[: 2 + len(arrays)], refs[-1])

    return pl.pallas_call(
        kernel,
        grid=(width // tile,),
        in_specs=[
            pl.BlockSpec(memory_space=pltpu.SMEM),
            pl.BlockSpec((tokens, hidden), lambda i: (0, 0)),
        ]
        + [pl.BlockSpec((array.shape[0], tile), lambda i: (0, i)) for array in arrays]
        + [pl.BlockSpec(memory_space=pl.ANY)] * len(marks),
        out_specs=pl.BlockSpec((tile, hidden), lambda i: (i, 0)),
        out_shape=jax.ShapeDtypeStruct((width, hidden), jnp.bfloat16),
        cost_estimate=pl.CostEstimate(
            flops=2 * tokens * hidden * width,
            bytes_accessed=2 * (tokens * hidden + hidden * width + tokens * width),
            transcendentals=0,
        ),
        name="outer_product",
    )(jnp.full((1,), z, jnp.int32), gradients, *arrays, *marks)


def gather_over_yhi(local):
    y = lax.axis_index("yhi")
    rows, cols = local.shape
    pieces = [(0, local)]
    for k in (1, 3, 2):
        pieces.append((k, shift(local, "yhi", NY, k)))
    block = jnp.zeros((NY * rows, cols), local.dtype)
    for k, piece in pieces:
        block = lax.dynamic_update_slice(block, piece, (((y - k) & (NY - 1)) * rows, 0))
    return block


def ring_over_z(block):
    rows = block.shape[0]
    half = rows // 2
    held = [((0, 0, rows), block)]
    up, down = block, block
    marks = []
    for step in range(1, NZ // 2):
        up = shift(up, "z", NZ, 1)
        down = shift(down, "z", NZ, -1)
        held += [((-step, 0, rows), up), ((step, 0, rows), down)]
        if step in (1, 3):
            marks.append(mark(up, down))
    up = shift(up[:half], "z", NZ, 1)
    down = shift(down[half:], "z", NZ, -1)
    held += [((NZ // 2, 0, half), up), ((NZ // 2, half, half), down)]
    return held, marks


def shards(act_values, act_scales, grad_values, grad_scales, weight):
  grad_local = dequantize(grad_values, grad_scales)
  gradients = lax.all_gather(grad_local, ROW, axis=0, tiled=True)
  act_local = dequantize(act_values, act_scales)
  held, marks = ring_over_z(gather_over_yhi(act_local))
  partial = partial_product(gradients, weight)
  over_z = lax.psum_scatter(partial, "z", scatter_dimension=0, tiled=True)
  rows = act_local.shape[0]
  blocks = lax.all_to_all(over_z, "yhi", 0, 0, tiled=True).reshape(NY, rows, -1)
  summed = jnp.sum(blocks.astype(jnp.float32), axis=0).astype(jnp.bfloat16)
  weight_grad = outer_product(held, gradients, lax.axis_index("z"), marks)
  return (summed, weight_grad)


def solution(mesh):
    fine = Mesh(mesh.devices.reshape(2, 4, 2, NZ, NY), ROW + COL)
    placed = (P(COL, ROW), P(COL, ROW), P(ROW, COL), P(ROW, COL), P(ROW, COL))
    return jax.shard_map(
        shards,
        mesh=fine,
        in_specs=placed,
        out_specs=(P(COL, ROW), P(ROW, COL)),
        check_vma=False,
    )
```

```python
import jax
import jax.numpy as jnp
from jax import lax
from jax.experimental import pallas as pl
from jax.experimental.pallas import tpu as pltpu
from jax.sharding import Mesh, PartitionSpec as P


QB = 128
NY = 4
NZ = 8
ROW = ("ylo", "x", "core")
COL = ("z", "yhi")


def dequantize(values, scales):
    height, breadth = values.shape
    scaled = values.astype(jnp.float32).reshape(height, breadth // QB, QB) * scales[:, :, None]
    return scaled.reshape(height, breadth).astype(jnp.bfloat16)


def shift(array, axis, size, by):
    return lax.ppermute(array, axis, [(i, (i + by) % size) for i in range(size)])


def mark_kernel(*refs):
    refs[-1][...] = jnp.zeros_like(refs[-1])


def mark(*arrays):
    return pl.pallas_call(
        mark_kernel,
        in_specs=[pl.BlockSpec(memory_space=pl.ANY)] * len(arrays),
        out_shape=jax.ShapeDtypeStruct((8, 128), jnp.float32),
        cost_estimate=pl.CostEstimate(flops=0, bytes_accessed=4096, transcendentals=0),
        name="mark",
    )(*arrays)


def partial_kernel(grad_ref, weight_ref, *refs):
    out_ref = refs[-1]
    out_ref[...] = lax.dot_general(
        grad_ref[...], weight_ref[...], (((1,), (1,)), ((), ())), preferred_element_type=jnp.float32
    ).astype(out_ref.dtype)


def partial_product(gradients, weight, marks, tile=256):
    tokens, hidden = gradients.shape
    width = weight.shape[0]
    return pl.pallas_call(
        partial_kernel,
        grid=(tokens // tile,),
        in_specs=[
            pl.BlockSpec((tile, hidden), lambda i: (i, 0)),
            pl.BlockSpec((width, hidden), lambda i: (0, 0)),
        ]
        + [pl.BlockSpec(memory_space=pl.ANY)] * len(marks),
        out_specs=pl.BlockSpec((tile, width), lambda i: (i, 0)),
        out_shape=jax.ShapeDtypeStruct((tokens, width), jnp.bfloat16),
        cost_estimate=pl.CostEstimate(
            flops=2 * tokens * hidden * width,
            bytes_accessed=2 * (tokens * hidden + hidden * width + tokens * width),
            transcendentals=0,
        ),
        name="partial_product",
    )(gradients, weight, *marks)


def outer_kernel(keys, rows, place_ref, grad_ref, *refs):
    out_ref, acts_ref = refs[-2:]
    z, y = place_ref[0], place_ref[1]
    for key, act_ref in zip(keys, refs):
        for j, (hop, lane) in enumerate(key):
            start = (((z + hop) & (NZ - 1)) * NY + ((y + lane) & (NY - 1))) * rows
            acts_ref[pl.ds(pl.multiple_of(start, rows), rows), :] = act_ref[j * rows : (j + 1) * rows, :]
    out_ref[...] = lax.dot_general(
        acts_ref[...], grad_ref[...], (((0,), (0,)), ((), ())), preferred_element_type=jnp.float32
    ).astype(out_ref.dtype)


def outer_product(place, gradients, held, marks, tile=256):
    tokens, hidden = gradients.shape
    width = held[0][1].shape[1]
    keys = [key for key, _ in held]
    arrays = [array for _, array in held]

    def kernel(*refs):
        outer_kernel(keys, tokens // (NZ * NY), *refs[: 2 + len(arrays)], *refs[-2:])

    return pl.pallas_call(
        kernel,
        grid=(width // tile,),
        in_specs=[
            pl.BlockSpec(memory_space=pltpu.SMEM),
            pl.BlockSpec((tokens, hidden), lambda i: (0, 0)),
        ]
        + [pl.BlockSpec((array.shape[0], tile), lambda i: (0, i)) for array in arrays]
        + [pl.BlockSpec(memory_space=pl.ANY)] * len(marks),
        out_specs=pl.BlockSpec((tile, hidden), lambda i: (i, 0)),
        out_shape=jax.ShapeDtypeStruct((width, hidden), jnp.bfloat16),
        scratch_shapes=[pltpu.VMEM((tokens, tile), jnp.bfloat16)],
        cost_estimate=pl.CostEstimate(
            flops=2 * tokens * hidden * width,
            bytes_accessed=2 * (tokens * hidden + hidden * width + tokens * width),
            transcendentals=0,
        ),
        name="outer_product",
    )(place, gradients, *arrays, *marks)


def gather_acts(local):
    rows = local.shape[0]
    opposite = shift(local, "yhi", NY, NY // 2)
    ups, downs = [jnp.concatenate([local, opposite], axis=0)], []
    downs.append(ups[0])
    for _ in range(1, NZ // 2):
        ups.append(shift(ups[-1], "z", NZ, 1))
        downs.append(shift(downs[-1], "z", NZ, -1))
    ups.append(shift(ups[-1], "z", NZ, 1))
    ring = [(0, ups[0])]
    for step in range(1, NZ // 2):
        ring += [(-step, ups[step]), (step, downs[step])]
    ring.append((NZ // 2, ups[-1]))
    column = jnp.concatenate([array[:rows] for _, array in ring], axis=0)
    left = shift(column, "yhi", NY, 1)
    right = shift(column, "yhi", NY, -1)
    hops = [hop for hop, _ in ring]
    held = [([(hop, -1) for hop in hops], left), ([(hop, 1) for hop in hops], right)]
    held += [([(hop, 0), (hop, NY // 2)], array) for hop, array in ring]
    return held, [mark(ups[2], downs[2])]


def shards(act_values, act_scales, grad_values, grad_scales, weight):
    place = jnp.stack([lax.axis_index("z"), lax.axis_index("yhi")]).astype(jnp.int32)
    rows = act_values.shape[0]
    grad_local = dequantize(grad_values, grad_scales)
    gradients = lax.all_gather(grad_local, ROW, axis=0, tiled=True)
    held, marks = gather_acts(dequantize(act_values, act_scales))
    partial = partial_product(gradients, weight, [])
    over_z = lax.psum_scatter(partial, "z", scatter_dimension=0, tiled=True)
    blocks = lax.all_to_all(over_z, "yhi", 0, 0, tiled=True).reshape(NY, rows, -1)
    summed = jnp.sum(blocks.astype(jnp.float32), axis=0).astype(jnp.bfloat16)
    weight_grad = outer_product(place, gradients, held, marks)
    return (summed, weight_grad)


def solution(mesh):
    fine = Mesh(mesh.devices.reshape(2, 4, 2, NZ, NY), ROW + COL)
    placed = (P(COL, ROW), P(COL, ROW), P(ROW, COL), P(ROW, COL), P(ROW, COL))
    return jax.shard_map(
        shards,
        mesh=fine,
        in_specs=placed,
        out_specs=(P(COL, ROW), P(ROW, COL)),
        check_vma=False,
    )
```

```python
import jax
import jax.numpy as jnp
from jax import lax
from jax.experimental import pallas as pl
from jax.experimental.pallas import tpu as pltpu
from jax.sharding import Mesh, PartitionSpec as P


QB = 128
NY = 4
NZ = 8
ROW = ("ylo", "x", "core")
COL = ("z", "yhi")


def dequantize_kernel(values_ref, scales_ref, out_ref):
    scales = scales_ref[...].T
    for j in range(scales.shape[1]):
        part = slice(j * QB, (j + 1) * QB)
        out_ref[:, part] = (values_ref[:, part].astype(jnp.float32) * scales[:, j : j + 1]).astype(out_ref.dtype)


def dequantize(values, scales):
    return pl.pallas_call(
        dequantize_kernel,
        out_shape=jax.ShapeDtypeStruct(values.shape, jnp.bfloat16),
        cost_estimate=pl.CostEstimate(flops=values.size, bytes_accessed=4 * values.size, transcendentals=0),
        name="dequantize",
    )(values, scales.T)


def shift(array, axis, size, by):
    return lax.ppermute(array, axis, [(i, (i + by) % size) for i in range(size)])


def mark_kernel(*refs):
    refs[-1][...] = jnp.zeros_like(refs[-1])


def mark(*arrays):
    return pl.pallas_call(
        mark_kernel,
        in_specs=[pl.BlockSpec(memory_space=pl.ANY)] * len(arrays),
        out_shape=jax.ShapeDtypeStruct((8, 128), jnp.float32),
        cost_estimate=pl.CostEstimate(flops=0, bytes_accessed=4096, transcendentals=0),
        name="mark",
    )(*arrays)


def partial_kernel(grad_ref, weight_ref, *refs):
    out_ref = refs[-1]
    out_ref[...] = lax.dot_general(
        grad_ref[...], weight_ref[...], (((1,), (1,)), ((), ())), preferred_element_type=jnp.float32
    ).astype(out_ref.dtype)


def partial_product(gradients, weight, marks, tile=512):
    tokens, hidden = gradients.shape
    width = weight.shape[0]
    return pl.pallas_call(
        partial_kernel,
        grid=(tokens // tile,),
        in_specs=[
            pl.BlockSpec((tile, hidden), lambda i: (i, 0)),
            pl.BlockSpec((width, hidden), lambda i: (0, 0)),
        ]
        + [pl.BlockSpec(memory_space=pl.ANY)] * len(marks),
        out_specs=pl.BlockSpec((tile, width), lambda i: (i, 0)),
        out_shape=jax.ShapeDtypeStruct((tokens, width), jnp.bfloat16),
        cost_estimate=pl.CostEstimate(
            flops=2 * tokens * hidden * width,
            bytes_accessed=2 * (tokens * hidden + hidden * width + tokens * width),
            transcendentals=0,
        ),
        name="partial_product",
    )(gradients, weight, *marks)


def outer_kernel(keys, rows, place_ref, grad_ref, *refs):
    out_ref, acts_ref = refs[-2:]
    z, y = place_ref[0], place_ref[1]
    for key, act_ref in zip(keys, refs):
        for j, (hop, lane) in enumerate(key):
            start = (((z + hop) & (NZ - 1)) * NY + ((y + lane) & (NY - 1))) * rows
            acts_ref[pl.ds(pl.multiple_of(start, rows), rows), :] = act_ref[j * rows : (j + 1) * rows, :]
    out_ref[...] = lax.dot_general(
        acts_ref[...], grad_ref[...], (((0,), (0,)), ((), ())), preferred_element_type=jnp.float32
    ).astype(out_ref.dtype)


def outer_product(place, gradients, held, marks, tile=256):
    tokens, hidden = gradients.shape
    width = held[0][1].shape[1]
    keys = [key for key, _ in held]
    arrays = [array for _, array in held]

    def kernel(*refs):
        outer_kernel(keys, tokens // (NZ * NY), *refs[: 2 + len(arrays)], *refs[-2:])

    return pl.pallas_call(
        kernel,
        grid=(width // tile,),
        in_specs=[
            pl.BlockSpec(memory_space=pltpu.SMEM),
            pl.BlockSpec((tokens, hidden), lambda i: (0, 0)),
        ]
        + [pl.BlockSpec((array.shape[0], tile), lambda i: (0, i)) for array in arrays]
        + [pl.BlockSpec(memory_space=pl.ANY)] * len(marks),
        out_specs=pl.BlockSpec((tile, hidden), lambda i: (i, 0)),
        out_shape=jax.ShapeDtypeStruct((width, hidden), jnp.bfloat16),
        scratch_shapes=[pltpu.VMEM((tokens, tile), jnp.bfloat16)],
        cost_estimate=pl.CostEstimate(
            flops=2 * tokens * hidden * width,
            bytes_accessed=2 * (tokens * hidden + hidden * width + tokens * width),
            transcendentals=0,
        ),
        name="outer_product",
    )(place, gradients, *arrays, *marks)


def gather_acts(local):
    rows = local.shape[0]
    opposite = shift(local, "yhi", NY, NY // 2)
    ups, downs = [jnp.concatenate([local, opposite], axis=0)], []
    downs.append(ups[0])
    for _ in range(1, NZ // 2):
        ups.append(shift(ups[-1], "z", NZ, 1))
        downs.append(shift(downs[-1], "z", NZ, -1))
    ups.append(shift(ups[-1], "z", NZ, 1))
    ring = [(0, ups[0])]
    for step in range(1, NZ // 2):
        ring += [(-step, ups[step]), (step, downs[step])]
    ring.append((NZ // 2, ups[-1]))
    column = jnp.concatenate([array[:rows] for _, array in ring], axis=0)
    left = shift(column, "yhi", NY, 1)
    right = shift(column, "yhi", NY, -1)
    hops = [hop for hop, _ in ring]
    held = [([(hop, -1) for hop in hops], left), ([(hop, 1) for hop in hops], right)]
    held += [([(hop, 0), (hop, NY // 2)], array) for hop, array in ring]
    return held, [mark(ups[2], downs[2])]


def shards(act_values, act_scales, grad_values, grad_scales, weight):
    place = jnp.stack([lax.axis_index("z"), lax.axis_index("yhi")]).astype(jnp.int32)
    rows = act_values.shape[0]
    grad_local = dequantize(grad_values, grad_scales)
    gradients = lax.all_gather(grad_local, ROW, axis=0, tiled=True)
    held, marks = gather_acts(dequantize(act_values, act_scales))
    partial = partial_product(gradients, weight, [])
    over_z = lax.psum_scatter(partial, "z", scatter_dimension=0, tiled=True)
    blocks = lax.all_to_all(over_z, "yhi", 0, 0, tiled=True).reshape(NY, rows, -1)
    summed = jnp.sum(blocks.astype(jnp.float32), axis=0).astype(jnp.bfloat16)
    weight_grad = outer_product(place, gradients, held, marks)
    return (summed, weight_grad)


def solution(mesh):
    fine = Mesh(mesh.devices.reshape(2, 4, 2, NZ, NY), ROW + COL)
    placed = (P(COL, ROW), P(COL, ROW), P(ROW, COL), P(ROW, COL), P(ROW, COL))
    return jax.shard_map(
        shards,
        mesh=fine,
        in_specs=placed,
        out_specs=(P(COL, ROW), P(ROW, COL)),
        check_vma=False,
    )
```
